32 devices in a mesh: outer: 8 (over z, x), inner: 4 (over y, core).
Axes of the slice: x: 2, y: 2, z: 4, core: 2. Of those that a mesh axis runs over, the one named last changes fastest.
Arguments:
- state_vector: float32 [2, 8, 4, 32768], P(None, 'outer', 'inner'), may hold values from -6 to 6
- gate_matrices: float32 [4, 2, 128, 128], replicated, may hold values from -4 to 4, as said below
Outputs:
- final_state: float32 [2, 8, 4, 32768], P(None, 'outer', 'inner')
- state_rms: float32 [], replicated
The draws below stay inside these ranges and needn't reach their ends.
Inputs may be any that keep to these rules, and one draw needn't show every extreme that they name: `gate_matrices`: each gate is a general complex matrix, not necessarily unitary.
All inputs are finite; a program needn't handle non-finite values.
Results may differ from the reference program's by a relative error of at most 0.000098.
Values sent between devices are 32-bit elements; how exact they have to be, the bound alone decides.
A program may use at most 64 MiB of HBM per device.

```python
import math
import jax
import jax.numpy as jnp
from jax import lax

GATE_QUBITS = 7
AMP_DEV = 32768
N_OUTER = 8
N_INNER = 4


def draw_gate_matrices(key, part):
    size_dim = 2 ** GATE_QUBITS
    key_real, key_imag, key_rough, key_phase = jax.random.split(key, 4)
    noise_real = jnp.clip(jax.random.normal(key_real, (4, size_dim, size_dim), jnp.float32), -3.5, 3.5)
    noise_imag = jnp.clip(jax.random.normal(key_imag, (4, size_dim, size_dim), jnp.float32), -3.5, 3.5)
    qubit_position = jnp.arange(size_dim, dtype=jnp.float32) / (size_dim - 1)
    rising = 3.0 ** qubit_position / 1.82
    roughness = jax.random.uniform(key_rough, (4, size_dim, 1), jnp.float32, 0.8, 1.25)
    row_scale = rising[None, :, None] * roughness
    phase_angle = jax.random.uniform(key_phase, (4, size_dim), jnp.float32, -math.pi, math.pi)
    eye_mat = jnp.eye(size_dim, dtype=jnp.float32)
    stride_spread = 0.4 / math.sqrt(size_dim)
    real_part = row_scale * (eye_mat[None] * jnp.cos(phase_angle)[:, None, :] + stride_spread * noise_real)
    imag_part = row_scale * (eye_mat[None] * jnp.sin(phase_angle)[:, None, :] + stride_spread * noise_imag)
    return jnp.stack([real_part, imag_part], axis=1).astype(jnp.float32)


def shard_levels(key, extent, pieces, least, top_value):
    factor_of = 1.0
    for axis_at, blocks in pieces:
        heights = jax.random.uniform(jax.random.fold_in(jax.random.fold_in(key, 6), axis_at), (blocks,), jnp.float32, least / len(pieces), top_value / len(pieces))
        factor_of = factor_of * jnp.repeat(jnp.exp(heights), extent[axis_at] // blocks).reshape((-1,) + (1,) * (len(extent) - 1 - axis_at))
    return factor_of


def noise(rng, dims, width, limit, cuts=(), held_as=jnp.bfloat16):
    array = jax.random.normal(rng, dims, jnp.float32) * width
    if len(cuts) > 0:
        array = shard_levels(rng, dims, cuts, -0.22, 0.18) * array
    return jnp.clip(array, min=-limit, max=limit).astype(held_as)


def setup_inputs(seed: int = 0) -> dict:
    key_list = jax.random.split(jax.random.key(seed), 3)
    state_vector = noise(key_list[0], (2, N_OUTER, N_INNER, AMP_DEV), 1.0, 6.0, ((1, 8), (2, 4)), jnp.float32)
    gate_matrices = draw_gate_matrices(jax.random.fold_in(key_list[2], 71), 0)
    return {"state_vector": state_vector, "gate_matrices": gate_matrices}


def rows_apply(matrix_pair, blocks):

    def product(gate_matrix, value_entries):
        return jnp.einsum('ng,wgy->wny', gate_matrix, value_entries, precision=lax.Precision.HIGHEST)
    real_out = product(matrix_pair[0], blocks[0]) - product(matrix_pair[1], blocks[1])
    imag_out = product(matrix_pair[0], blocks[1]) + product(matrix_pair[1], blocks[0])
    return jnp.stack([real_out, imag_out])

def low_apply(matrix_pair, blocks):

    def product(gate_matrix, value_entries):
        return jnp.einsum('km,xm->xk', gate_matrix, value_entries, precision=lax.Precision.HIGHEST)
    real_out = product(matrix_pair[0], blocks[0]) - product(matrix_pair[1], blocks[1])
    imag_out = product(matrix_pair[0], blocks[1]) + product(matrix_pair[1], blocks[0])
    return jnp.stack([real_out, imag_out])

def reference(state_vector, gate_matrices):
    outer_count = state_vector.shape[1]
    inner_count = state_vector.shape[2]
    amp_count = state_vector.shape[3]
    gate_dim = gate_matrices.shape[2]
    width_low = amp_count // gate_dim
    amplitude_values = rows_apply(gate_matrices[0], state_vector.reshape(2, -1, gate_dim, gate_dim))
    outer_rest = gate_dim // outer_count
    amplitude_values = amplitude_values.reshape(2, outer_count, inner_count, outer_count, outer_rest, width_low)
    amplitude_values = amplitude_values.transpose(0, 2, 3, 1, 4, 5).reshape(2, inner_count * outer_count, gate_dim, width_low)
    amplitude_values = rows_apply(gate_matrices[1], amplitude_values)
    amplitude_values = amplitude_values.reshape(2, inner_count, outer_count, outer_count, outer_rest, width_low)
    amplitude_values = amplitude_values.transpose(0, 3, 1, 2, 4, 5)
    inner_rest = gate_dim // inner_count
    amplitude_values = amplitude_values.reshape(2, outer_count, inner_count, inner_count, inner_rest, width_low)
    amplitude_values = amplitude_values.transpose(0, 1, 3, 2, 4, 5).reshape(2, outer_count * inner_count, gate_dim, width_low)
    amplitude_values = rows_apply(gate_matrices[2], amplitude_values)
    amplitude_values = amplitude_values.reshape(2, outer_count, inner_count, inner_count, inner_rest, width_low)
    amplitude_values = amplitude_values.transpose(0, 1, 3, 2, 4, 5)
    amplitude_values = low_apply(gate_matrices[3], amplitude_values.reshape(2, -1, gate_dim))
    amplitude_values = amplitude_values.reshape(2, outer_count, inner_count, amp_count)
    total_sum = jnp.sum(amplitude_values * amplitude_values)
    amplitude_total = outer_count * inner_count * amp_count
    root_mean = jnp.sqrt(total_sum / amplitude_total)
    final_state = amplitude_values / root_mean
    return (final_state, root_mean)
```

```python
import functools

import jax
import jax.numpy as jnp
from jax import lax
from jax.experimental import pallas as pl
from jax.experimental.pallas import tpu as pltpu
from jax.sharding import PartitionSpec as P

MESH = pl.DeviceIdType.MESH


def halves(values):
    high = values.astype(jnp.bfloat16)
    low = (values - high.astype(jnp.float32)).astype(jnp.bfloat16)
    return high, low


def product(left, right, dims):
    def one(a, b):
        return lax.dot_general(a, b, (dims, ((), ())), preferred_element_type=jnp.float32)

    return one(left[0], right[0]) + (one(left[0], right[1]) + one(left[1], right[0]))


def complex_matrix(real, imag):
    top = jnp.concatenate([real, -imag], axis=1)
    bottom = jnp.concatenate([imag, real], axis=1)
    return halves(jnp.concatenate([top, bottom], axis=0))


def spread(position, count):
    return (position % 2) * (count // 2) + position // 2


def kernel(
    n_outer, n_inner, chunks, state, gates, out, rms,
    sent_a, held_a, sent_b, held_b, sent_c, held_c, part, sums,
    send_a, recv_a, send_b, recv_b, send_c, recv_c, send_s, recv_s,
):
    dim = gates.shape[2]
    passive = state.shape[1] // dim
    sub = passive // chunks
    step = dim // chunks
    rows_outer = dim // n_outer * sub
    rows_inner = dim // n_inner * sub
    ratio = n_outer // n_inner
    n_all = n_outer * n_inner
    outer, inner = lax.axis_index("outer"), lax.axis_index("inner")
    me = outer * n_inner + inner

    def block(ref, chunk, at, rows):
        return ref.at[chunk, :, pl.ds(pl.multiple_of(at * rows, rows), rows), :]

    def remote(src, dst, send, recv, target):
        return pltpu.make_async_remote_copy(
            src_ref=src, dst_ref=dst, send_sem=send, recv_sem=recv,
            device_id=target, device_id_type=MESH,
        )

    def everyone(act):
        def body(k, carry):
            peer = (me + k) % n_all
            act(k, peer, (peer // n_inner, peer % n_inner))
            return carry

        lax.fori_loop(1, n_all, body, 0)

    barrier = pltpu.get_barrier_semaphore()

    def greet(k, peer, target):
        pl.semaphore_signal(barrier, inc=1, device_id=target, device_id_type=MESH)

    everyone(greet)

    def load(ref, chunk):
        return jnp.concatenate(
            [
                jnp.concatenate(
                    [ref[chunk, c, pl.ds(b, dim, stride=sub), :] for b in range(sub)], axis=1
                )
                for c in range(2)
            ],
            axis=0,
        )

    def store(ref, chunk, values):
        for c in range(2):
            for b in range(sub):
                ref[chunk, c, pl.ds(b, dim, stride=sub), :] = values[
                    c * dim : (c + 1) * dim, b * dim : (b + 1) * dim
                ]

    def low_gate(matrix, values):
        columns = []
        for b in range(sub):
            both = values[:, b * dim : (b + 1) * dim]
            wide = jnp.concatenate([both[:dim], both[dim:]], axis=1)
            wide = product(halves(wide), matrix, ((1,), (1,)))
            columns.append(jnp.concatenate([wide[:, :dim], wide[:, dim:]], axis=0))
        return jnp.concatenate(columns, axis=1)

    first = halves(
        jnp.concatenate(
            [
                jnp.concatenate(
                    [state[c, w * dim : (w + 1) * dim, :] for w in range(passive)], axis=1
                )
                for c in range(2)
            ],
            axis=0,
        )
    )

    def trade_a(chunk):
        for k in range(1, n_outer):
            to = (outer + k) % n_outer
            remote(
                block(sent_a, chunk, spread(to, n_outer), rows_outer),
                block(held_a, chunk, outer, rows_outer),
                send_a.at[chunk, to], recv_a.at[chunk, outer], (to, inner),
            ).start()
        pltpu.make_async_copy(
            block(sent_a, chunk, spread(outer, n_outer), rows_outer),
            block(held_a, chunk, outer, rows_outer),
            recv_a.at[chunk, outer],
        ).start()

    for chunk in range(chunks):
        pick = pl.ds(chunk, step, stride=chunks)
        matrix = complex_matrix(gates[0, 0, pick, :], gates[0, 1, pick, :])
        values = product(matrix, first, ((1,), (0,)))
        for c in range(2):
            for w in range(passive):
                sent_a[chunk, c, w * step : (w + 1) * step, :] = values[
                    c * step : (c + 1) * step, w * dim : (w + 1) * dim
                ]
        if chunk == 0:
            pl.semaphore_wait(barrier, n_all - 1)
        trade_a(chunk)

    low_matrix = complex_matrix(gates[3, 0], gates[3, 1])
    matrix = complex_matrix(gates[1, 0], gates[1, 1])
    mine = spread(outer, n_outer)
    column, within = mine // ratio, mine % ratio
    slot = inner * ratio + within
    for chunk in range(chunks):
        for k in range(n_outer):
            spot = block(held_a, chunk, k, rows_outer)
            remote(spot, spot, send_a.at[chunk, k], recv_a.at[chunk, k], (outer, inner)).wait_recv()
        values = low_gate(low_matrix, load(held_a, chunk))
        store(sent_b, chunk, product(matrix, halves(values), ((1,), (0,))))
        for k in range(n_outer):
            to = (outer + k) % n_outer
            src = block(sent_b, chunk, to, rows_outer)
            dst = block(held_b, chunk, slot, rows_outer)
            copy = remote(
                src, dst, send_b.at[chunk, to], recv_b.at[chunk, slot], (to, column)
            )
            if k > 0:
                copy.start()
            else:
                pl.when(column != inner)(copy.start)
                pl.when(column == inner)(
                    pltpu.make_async_copy(src, dst, recv_b.at[chunk, slot]).start
                )

    matrix = complex_matrix(gates[2, 0], gates[2, 1])
    total = jnp.zeros((8, dim), jnp.float32)
    for chunk in range(chunks):
        for k in range(n_outer):
            spot = block(held_b, chunk, k, rows_outer)
            remote(spot, spot, send_b.at[chunk, k], recv_b.at[chunk, k], (outer, inner)).wait_recv()
        values = product(matrix, halves(load(held_b, chunk)), ((1,), (0,)))
        store(sent_c, chunk, values)
        for k in range(1, n_inner):
            to = (inner + k) % n_inner
            remote(
                block(sent_c, chunk, to, rows_inner),
                block(held_c, chunk, inner, rows_inner),
                send_c.at[chunk, to], recv_c.at[chunk, inner], (outer, to),
            ).start()
        pltpu.make_async_copy(
            block(sent_c, chunk, inner, rows_inner),
            block(held_c, chunk, inner, rows_inner),
            recv_c.at[chunk, inner],
        ).start()
        for b in range(sub):
            piece = values[:, b * dim : (b + 1) * dim]
            total = total + jnp.sum((piece * piece).reshape(-1, 8, dim), axis=0)

    part[...] = total
    sums[me] = total

    def share(k, peer, target):
        remote(part, sums.at[me], send_s.at[k], recv_s.at[k], target).start()

    everyone(share)

    def arrived(k, peer, target):
        remote(part, sums.at[me], send_s.at[k], recv_s.at[k], target).wait_send()
        source = (me + n_all - k) % n_all
        remote(part, sums.at[source], send_s.at[k], recv_s.at[k], target).wait_recv()

    everyone(arrived)
    whole = jnp.sum(jnp.sum(sums[...], axis=0), axis=(0, 1), keepdims=True)
    count = n_all * state.shape[1] * dim
    root = jnp.sqrt(whole / count)
    rms[...] = root
    scale = jnp.broadcast_to(root, (8, dim))
    for chunk in range(chunks):
        for k in range(n_inner):
            spot = block(held_c, chunk, k, rows_inner)
            remote(spot, spot, send_c.at[chunk, k], recv_c.at[chunk, k], (outer, inner)).wait_recv()
        for c in range(2):
            values = held_c[chunk, c].reshape(-1, 8, dim) / scale[None]
            out[c, pl.ds(chunk, dim * sub, stride=chunks), :] = values.reshape(-1, dim)

    for chunk in range(chunks):
        for k in range(1, n_outer):
            to = (outer + k) % n_outer
            spot = block(sent_a, chunk, to, rows_outer)
            remote(spot, spot, send_a.at[chunk, to], recv_a.at[chunk, to], (to, inner)).wait_send()
        for k in range(n_outer):
            to = (outer + k) % n_outer
            spot = block(sent_b, chunk, to, rows_outer)
            copy = remote(spot, spot, send_b.at[chunk, to], recv_b.at[chunk, to], (to, column))
            if k > 0:
                copy.wait_send()
            else:
                pl.when(column != inner)(copy.wait_send)
        for k in range(1, n_inner):
            to = (inner + k) % n_inner
            spot = block(sent_c, chunk, to, rows_inner)
            remote(spot, spot, send_c.at[chunk, to], recv_c.at[chunk, to], (outer, to)).wait_send()


def shards(n_outer, n_inner, state_vector, gate_matrices):
    dim = gate_matrices.shape[2]
    amp_count = state_vector.shape[3]
    rows = amp_count // dim
    passive = rows // dim
    chunks = passive if (dim // n_outer) % 8 == 0 else 1
    held = pltpu.VMEM((chunks, 2, rows // chunks, dim), jnp.float32)
    n_all = n_outer * n_inner
    dma = pltpu.SemaphoreType.DMA
    vmem = pl.BlockSpec(memory_space=pltpu.VMEM)
    final_state, root = pl.pallas_call(
        functools.partial(kernel, n_outer, n_inner, chunks),
        out_shape=(
            jax.ShapeDtypeStruct((2, rows, dim), jnp.float32),
            jax.ShapeDtypeStruct((1, 1), jnp.float32),
        ),
        in_specs=[vmem, vmem],
        out_specs=(vmem, vmem),
        scratch_shapes=[held] * 6
        + [pltpu.VMEM((8, dim), jnp.float32), pltpu.VMEM((n_all, 8, dim), jnp.float32)]
        + [dma((chunks, n_outer))] * 4
        + [dma((chunks, n_inner))] * 2
        + [dma((n_all,))] * 2,
        compiler_params=pltpu.CompilerParams(collective_id=0, has_side_effects=True),
    )(state_vector.reshape(2, rows, dim), gate_matrices)
    return final_state.reshape(state_vector.shape), root.reshape(())


def solution(mesh):
    in_specs = (P(None, "outer", "inner", None), P())
    out_specs = (P(None, "outer", "inner", None), P())
    body = functools.partial(shards, mesh.shape["outer"], mesh.shape["inner"])
    return jax.shard_map(body, mesh=mesh, in_specs=in_specs, out_specs=out_specs, check_vma=False)
```

```python
import functools

import jax
import jax.numpy as jnp
from jax import lax
from jax.experimental import pallas as pl
from jax.experimental.pallas import tpu as pltpu
from jax.sharding import PartitionSpec as P

MESH = pl.DeviceIdType.MESH
LIMIT = 16 * 1024 * 1024


def halves(values):
    high = values.astype(jnp.bfloat16)
    low = (values - high.astype(jnp.float32)).astype(jnp.bfloat16)
    return high, low


def product(left, right, dims):
    def one(a, b):
        return lax.dot_general(a, b, (dims, ((), ())), preferred_element_type=jnp.float32)

    return one(left[0], right[0]) + (one(left[0], right[1]) + one(left[1], right[0]))


def complex_matrix(real, imag):
    top = jnp.concatenate([real, -imag], axis=1)
    bottom = jnp.concatenate([imag, real], axis=1)
    return halves(jnp.concatenate([top, bottom], axis=0))


def spread(position, count):
    return (position % 2) * (count // 2) + position // 2


def kernel(
    n_outer, n_inner, chunks, state, gates, held_c, sums,
    sent_a, held_a, sent_b, held_b, sent_c, part,
    send_a, recv_a, send_b, recv_b, send_c, recv_c, send_s, recv_s,
):
    dim = gates.shape[2]
    passive = state.shape[1] // dim
    sub = passive // chunks
    step = dim // chunks
    rows_outer = dim // n_outer * sub
    rows_inner = dim // n_inner * sub
    ratio = n_outer // n_inner
    n_all = n_outer * n_inner
    outer, inner = lax.axis_index("outer"), lax.axis_index("inner")
    me = outer * n_inner + inner

    def block(ref, chunk, at, rows):
        return ref.at[chunk, :, pl.ds(pl.multiple_of(at * rows, rows), rows), :]

    def remote(src, dst, send, recv, target):
        return pltpu.make_async_remote_copy(
            src_ref=src, dst_ref=dst, send_sem=send, recv_sem=recv,
            device_id=target, device_id_type=MESH,
        )

    def everyone(act):
        def body(k, carry):
            peer = (me + k) % n_all
            act(k, peer, (peer // n_inner, peer % n_inner))
            return carry

        lax.fori_loop(1, n_all, body, 0)

    barrier = pltpu.get_barrier_semaphore()

    def greet(k, peer, target):
        pl.semaphore_signal(barrier, inc=1, device_id=target, device_id_type=MESH)

    everyone(greet)

    def load(ref, chunk):
        return jnp.concatenate(
            [
                jnp.concatenate(
                    [ref[chunk, c, pl.ds(b, dim, stride=sub), :] for b in range(sub)], axis=1
                )
                for c in range(2)
            ],
            axis=0,
        )

    def store(ref, chunk, values):
        for c in range(2):
            for b in range(sub):
                ref[chunk, c, pl.ds(b, dim, stride=sub), :] = values[
                    c * dim : (c + 1) * dim, b * dim : (b + 1) * dim
                ]

    def low_gate(matrix, values):
        columns = []
        for b in range(sub):
            both = values[:, b * dim : (b + 1) * dim]
            wide = jnp.concatenate([both[:dim], both[dim:]], axis=1)
            wide = product(halves(wide), matrix, ((1,), (1,)))
            columns.append(jnp.concatenate([wide[:, :dim], wide[:, dim:]], axis=0))
        return jnp.concatenate(columns, axis=1)

    first = halves(
        jnp.concatenate(
            [
                jnp.concatenate(
                    [state[c, w * dim : (w + 1) * dim, :] for w in range(passive)], axis=1
                )
                for c in range(2)
            ],
            axis=0,
        )
    )

    def trade_a(chunk):
        for k in range(1, n_outer):
            to = (outer + k) % n_outer
            remote(
                block(sent_a, chunk, spread(to, n_outer), rows_outer),
                block(held_a, chunk, outer, rows_outer),
                send_a.at[chunk, to], recv_a.at[chunk, outer], (to, inner),
            ).start()
        pltpu.make_async_copy(
            block(sent_a, chunk, spread(outer, n_outer), rows_outer),
            block(held_a, chunk, outer, rows_outer),
            recv_a.at[chunk, outer],
        ).start()

    for chunk in range(chunks):
        pick = pl.ds(chunk, step, stride=chunks)
        matrix = complex_matrix(gates[0, 0, pick, :], gates[0, 1, pick, :])
        values = product(matrix, first, ((1,), (0,)))
        for c in range(2):
            for w in range(passive):
                sent_a[chunk, c, w * step : (w + 1) * step, :] = values[
                    c * step : (c + 1) * step, w * dim : (w + 1) * dim
                ]
        if chunk == 0:
            pl.semaphore_wait(barrier, n_all - 1)
        trade_a(chunk)

    low_matrix = complex_matrix(gates[3, 0], gates[3, 1])
    matrix = complex_matrix(gates[1, 0], gates[1, 1])
    mine = spread(outer, n_outer)
    column, within = mine // ratio, mine % ratio
    slot = inner * ratio + within
    for chunk in range(chunks):
        for k in range(n_outer):
            spot = block(held_a, chunk, k, rows_outer)
            remote(spot, spot, send_a.at[chunk, k], recv_a.at[chunk, k], (outer, inner)).wait_recv()
        values = low_gate(low_matrix, load(held_a, chunk))
        store(sent_b, chunk, product(matrix, halves(values), ((1,), (0,))))
        for k in range(n_outer):
            to = (outer + k) % n_outer
            src = block(sent_b, chunk, to, rows_outer)
            dst = block(held_b, chunk, slot, rows_outer)
            copy = remote(
                src, dst, send_b.at[chunk, to], recv_b.at[chunk, slot], (to, column)
            )
            if k > 0:
                copy.start()
            else:
                pl.when(column != inner)(copy.start)
                pl.when(column == inner)(
                    pltpu.make_async_copy(src, dst, recv_b.at[chunk, slot]).start
                )

    matrix = complex_matrix(gates[2, 0], gates[2, 1])
    total = jnp.zeros((1, dim), jnp.float32)
    own = pltpu.make_async_copy(part, sums.at[me], recv_s.at[0])

    def share(k, peer, target):
        remote(part, sums.at[me], send_s.at[k], recv_s.at[k], target).start()

    for chunk in range(chunks):
        for k in range(n_outer):
            spot = block(held_b, chunk, k, rows_outer)
            remote(spot, spot, send_b.at[chunk, k], recv_b.at[chunk, k], (outer, inner)).wait_recv()
        values = product(matrix, halves(load(held_b, chunk)), ((1,), (0,)))
        for b in range(sub):
            piece = values[:, b * dim : (b + 1) * dim]
            total = total + jnp.sum(piece * piece, axis=0, keepdims=True)
        if chunk == chunks - 1:
            part[...] = total
            everyone(share)
            own.start()
        store(sent_c, chunk, values)
        for k in range(1, n_inner):
            to = (inner + k) % n_inner
            remote(
                block(sent_c, chunk, to, rows_inner),
                block(held_c, chunk, inner, rows_inner),
                send_c.at[chunk, to], recv_c.at[chunk, inner], (outer, to),
            ).start()
        pltpu.make_async_copy(
            block(sent_c, chunk, inner, rows_inner),
            block(held_c, chunk, inner, rows_inner),
            recv_c.at[chunk, inner],
        ).start()

    def arrived(k, peer, target):
        remote(part, sums.at[me], send_s.at[k], recv_s.at[k], target).wait_send()
        source = (me + n_all - k) % n_all
        remote(part, sums.at[source], send_s.at[k], recv_s.at[k], target).wait_recv()

    everyone(arrived)
    own.wait()
    for chunk in range(chunks):
        for k in range(n_inner):
            spot = block(held_c, chunk, k, rows_inner)
            remote(spot, spot, send_c.at[chunk, k], recv_c.at[chunk, k], (outer, inner)).wait_recv()

    for chunk in range(chunks):
        for k in range(1, n_outer):
            to = (outer + k) % n_outer
            spot = block(sent_a, chunk, to, rows_outer)
            remote(spot, spot, send_a.at[chunk, to], recv_a.at[chunk, to], (to, inner)).wait_send()
        for k in range(n_outer):
            to = (outer + k) % n_outer
            spot = block(sent_b, chunk, to, rows_outer)
            copy = remote(spot, spot, send_b.at[chunk, to], recv_b.at[chunk, to], (to, column))
            if k > 0:
                copy.wait_send()
            else:
                pl.when(column != inner)(copy.wait_send)
        for k in range(1, n_inner):
            to = (inner + k) % n_inner
            spot = block(sent_c, chunk, to, rows_inner)
            remote(spot, spot, send_c.at[chunk, to], recv_c.at[chunk, to], (outer, to)).wait_send()


def finish(n_all, values, sums, out, rms):
    chunks, _, rows, dim = values.shape
    whole = jnp.sum(jnp.sum(sums[...], axis=0), axis=1, keepdims=True)
    root = jnp.sqrt(whole / (n_all * chunks * rows * dim))
    rms[...] = root
    scale = jnp.broadcast_to(root, (8, dim))
    for chunk in range(chunks):
        for c in range(2):
            scaled = values[chunk, c].reshape(-1, 8, dim) / scale[None]
            out[c, pl.ds(chunk, rows, stride=chunks), :] = scaled.reshape(-1, dim)


def shards(n_outer, n_inner, state_vector, gate_matrices):
    dim = gate_matrices.shape[2]
    amp_count = state_vector.shape[3]
    rows = amp_count // dim
    passive = rows // dim
    chunks = passive if (dim // n_outer) % 8 == 0 else 1
    held = pltpu.VMEM((chunks, 2, rows // chunks, dim), jnp.float32)
    n_all = n_outer * n_inner
    dma = pltpu.SemaphoreType.DMA
    vmem = pl.BlockSpec(memory_space=pltpu.VMEM)
    anywhere = pl.BlockSpec(memory_space=pl.ANY)
    values, sums = pl.pallas_call(
        functools.partial(kernel, n_outer, n_inner, chunks),
        out_shape=(
            jax.ShapeDtypeStruct((chunks, 2, rows // chunks, dim), jnp.float32),
            jax.ShapeDtypeStruct((n_all, 1, dim), jnp.float32),
        ),
        in_specs=[vmem, vmem],
        out_specs=(anywhere, anywhere),
        scratch_shapes=[held] * 5
        + [pltpu.VMEM((1, dim), jnp.float32)]
        + [dma((chunks, n_outer))] * 4
        + [dma((chunks, n_inner))] * 2
        + [dma((n_all,))] * 2,
        compiler_params=pltpu.CompilerParams(
            collective_id=0, has_side_effects=True, vmem_limit_bytes=LIMIT
        ),
    )(state_vector.reshape(2, rows, dim), gate_matrices)
    final_state, root = pl.pallas_call(
        functools.partial(finish, n_all),
        out_shape=(
            jax.ShapeDtypeStruct((2, rows, dim), jnp.float32),
            jax.ShapeDtypeStruct((1, 1), jnp.float32),
        ),
        in_specs=[vmem, vmem],
        out_specs=(vmem, vmem),
        compiler_params=pltpu.CompilerParams(vmem_limit_bytes=LIMIT),
    )(values, sums)
    return final_state.reshape(state_vector.shape), root.reshape(())


def solution(mesh):
    in_specs = (P(None, "outer", "inner", None), P())
    out_specs = (P(None, "outer", "inner", None), P())
    body = functools.partial(shards, mesh.shape["outer"], mesh.shape["inner"])
    return jax.shard_map(body, mesh=mesh, in_specs=in_specs, out_specs=out_specs, check_vma=False)
```

```python
import functools

import jax
import jax.numpy as jnp
from jax import lax
from jax.experimental import pallas as pl
from jax.experimental.pallas import tpu as pltpu
from jax.sharding import PartitionSpec as P

MESH = pl.DeviceIdType.MESH
TRADE_LIMIT = 56_150_000
LIMIT = 16 * 1024 * 1024


def halves(values):
    high = values.astype(jnp.bfloat16)
    low = (values - high.astype(jnp.float32)).astype(jnp.bfloat16)
    return high, low


def product(left, right, dims):
    def one(a, b):
        return lax.dot_general(a, b, (dims, ((), ())), preferred_element_type=jnp.float32)

    return one(left[0], right[0]) + (one(left[0], right[1]) + one(left[1], right[0]))


def complex_matrix(real, imag):
    top = jnp.concatenate([real, -imag], axis=1)
    bottom = jnp.concatenate([imag, real], axis=1)
    return halves(jnp.concatenate([top, bottom], axis=0))


def spread(position, count):
    return (position % 2) * (count // 2) + position // 2


def kernel(
    n_outer, n_inner, chunks, state_in, gates_in, held_c, sums,
    state, gates, sent_a, held_a, sent_b, held_b, sent_c, part, fetched,
    send_a, recv_a, send_b, recv_b, send_c, recv_c, send_s, recv_s,
):
    def fetch(at):
        if at == 0:
            return pltpu.make_async_copy(state_in, state, fetched.at[0])
        return pltpu.make_async_copy(gates_in.at[at - 1], gates.at[at - 1], fetched.at[at])

    for at in (0, 1, 4, 2, 3):
        fetch(at).start()
    dim = gates.shape[2]
    passive = state.shape[1] // dim
    sub = passive // chunks
    step = dim // chunks
    rows_outer = dim // n_outer * sub
    rows_inner = dim // n_inner * sub
    ratio = n_outer // n_inner
    n_all = n_outer * n_inner
    outer, inner = lax.axis_index("outer"), lax.axis_index("inner")
    me = outer * n_inner + inner

    def block(ref, chunk, at, rows):
        return ref.at[chunk, :, pl.ds(pl.multiple_of(at * rows, rows), rows), :]

    def remote(src, dst, send, recv, target):
        return pltpu.make_async_remote_copy(
            src_ref=src, dst_ref=dst, send_sem=send, recv_sem=recv,
            device_id=target, device_id_type=MESH,
        )

    def everyone(act):
        def body(k, carry):
            peer = (me + k) % n_all
            act(k, peer, (peer // n_inner, peer % n_inner))
            return carry

        lax.fori_loop(1, n_all, body, 0)

    barrier = pltpu.get_barrier_semaphore()

    for k in range(1, n_outer):
        pl.semaphore_signal(
            barrier, inc=1, device_id=((outer + k) % n_outer, inner), device_id_type=MESH
        )
    for k in range(1, n_inner):
        pl.semaphore_signal(
            barrier, inc=1, device_id=(outer, (inner + k) % n_inner), device_id_type=MESH
        )

    def load(ref, chunk):
        return jnp.concatenate(
            [
                jnp.concatenate(
                    [ref[chunk, c, pl.ds(b, dim, stride=sub), :] for b in range(sub)], axis=1
                )
                for c in range(2)
            ],
            axis=0,
        )

    def store(ref, chunk, values):
        for c in range(2):
            for b in range(sub):
                ref[chunk, c, pl.ds(b, dim, stride=sub), :] = values[
                    c * dim : (c + 1) * dim, b * dim : (b + 1) * dim
                ]

    def low_gate(values):
        rows = values.shape[0] // 2
        matrix = complex_matrix(gates[3, 0], gates[3, 1])
        columns = []
        for b in range(values.shape[1] // dim):
            both = values[:, b * dim : (b + 1) * dim]
            wide = jnp.concatenate([both[:rows], both[rows:]], axis=1)
            wide = product(halves(wide), matrix, ((1,), (1,)))
            columns.append(jnp.concatenate([wide[:, :dim], wide[:, dim:]], axis=0))
        return jnp.concatenate(columns, axis=1)

    far_first = sorted(range(n_outer), key=lambda k: abs(2 * k - n_outer))

    fetch(0).wait()
    fetch(1).wait()
    first = halves(
        jnp.concatenate(
            [
                jnp.concatenate(
                    [state[c, w * dim : (w + 1) * dim, :] for w in range(passive)], axis=1
                )
                for c in range(2)
            ],
            axis=0,
        )
    )

    def trade_a(chunk):
        for k in far_first[:-1]:
            to = (outer + k) % n_outer
            remote(
                block(sent_a, chunk, spread(to, n_outer), rows_outer),
                block(held_a, chunk, outer, rows_outer),
                send_a.at[chunk, to], recv_a.at[chunk, outer], (to, inner),
            ).start()
        pltpu.make_async_copy(
            block(sent_a, chunk, spread(outer, n_outer), rows_outer),
            block(held_a, chunk, outer, rows_outer),
            recv_a.at[chunk, outer],
        ).start()

    for chunk in range(chunks):
        pick = pl.ds(chunk, step, stride=chunks)
        matrix = complex_matrix(gates[0, 0, pick, :], gates[0, 1, pick, :])
        values = product(matrix, first, ((1,), (0,)))
        if chunk > 0:
            if chunk == 1:
                fetch(4).wait()
            values = low_gate(values)
        for c in range(2):
            for w in range(passive):
                sent_a[chunk, c, w * step : (w + 1) * step, :] = values[
                    c * step : (c + 1) * step, w * dim : (w + 1) * dim
                ]
        if chunk == 0:
            pl.semaphore_wait(barrier, n_outer + n_inner - 2)
        trade_a(chunk)

    fetch(2).wait()
    matrix = complex_matrix(gates[1, 0], gates[1, 1])
    mine = spread(outer, n_outer)
    column, within = mine // ratio, mine % ratio
    slot = inner * ratio + within
    for chunk in range(chunks):
        for k in range(n_outer):
            spot = block(held_a, chunk, k, rows_outer)
            remote(spot, spot, send_a.at[chunk, k], recv_a.at[chunk, k], (outer, inner)).wait_recv()
        values = halves(load(held_a, chunk))
        store(sent_b, chunk, product(matrix, values, ((1,), (0,))))
        for k in far_first:
            to = (outer + k) % n_outer
            src = block(sent_b, chunk, to, rows_outer)
            dst = block(held_b, chunk, slot, rows_outer)
            copy = remote(
                src, dst, send_b.at[chunk, to], recv_b.at[chunk, slot], (to, column)
            )
            if k > 0:
                copy.start()
            else:
                pl.when(column != inner)(copy.start)
                pl.when(column == inner)(
                    pltpu.make_async_copy(src, dst, recv_b.at[chunk, slot]).start
                )

    fetch(3).wait()
    matrix = complex_matrix(gates[2, 0], gates[2, 1])
    total = jnp.zeros((1, dim), jnp.float32)
    own = pltpu.make_async_copy(part, sums.at[me], recv_s.at[0])

    def share(k, peer, target):
        remote(part, sums.at[me], send_s.at[k], recv_s.at[k], target).start()

    for chunk in range(chunks):
        for k in range(n_outer):
            spot = block(held_b, chunk, k, rows_outer)
            remote(spot, spot, send_b.at[chunk, k], recv_b.at[chunk, k], (outer, inner)).wait_recv()
        values = product(matrix, halves(load(held_b, chunk)), ((1,), (0,)))
        if chunk == 0:
            if chunks == 1:
                fetch(4).wait()
            values = low_gate(values)
        for b in range(sub):
            piece = values[:, b * dim : (b + 1) * dim]
            total = total + jnp.sum(piece * piece, axis=0, keepdims=True)
        if chunk == chunks - 1:
            part[...] = total
            everyone(share)
            own.start()
        store(sent_c, chunk, values)
        for k in range(1, n_inner):
            to = (inner + k) % n_inner
            remote(
                block(sent_c, chunk, to, rows_inner),
                block(held_c, chunk, inner, rows_inner),
                send_c.at[chunk, to], recv_c.at[chunk, inner], (outer, to),
            ).start()
        pltpu.make_async_copy(
            block(sent_c, chunk, inner, rows_inner),
            block(held_c, chunk, inner, rows_inner),
            recv_c.at[chunk, inner],
        ).start()

    def arrived(k, peer, target):
        remote(part, sums.at[me], send_s.at[k], recv_s.at[k], target).wait_send()
        source = (me + n_all - k) % n_all
        remote(part, sums.at[source], send_s.at[k], recv_s.at[k], target).wait_recv()

    everyone(arrived)
    own.wait()
    for chunk in range(chunks):
        for k in range(n_inner):
            spot = block(held_c, chunk, k, rows_inner)
            remote(spot, spot, send_c.at[chunk, k], recv_c.at[chunk, k], (outer, inner)).wait_recv()

    for chunk in range(chunks):
        for k in range(1, n_outer):
            to = (outer + k) % n_outer
            spot = block(sent_a, chunk, to, rows_outer)
            remote(spot, spot, send_a.at[chunk, to], recv_a.at[chunk, to], (to, inner)).wait_send()
        for k in range(n_outer):
            to = (outer + k) % n_outer
            spot = block(sent_b, chunk, to, rows_outer)
            copy = remote(spot, spot, send_b.at[chunk, to], recv_b.at[chunk, to], (to, column))
            if k > 0:
                copy.wait_send()
            else:
                pl.when(column != inner)(copy.wait_send)
        for k in range(1, n_inner):
            to = (inner + k) % n_inner
            spot = block(sent_c, chunk, to, rows_inner)
            remote(spot, spot, send_c.at[chunk, to], recv_c.at[chunk, to], (outer, to)).wait_send()


def finish(n_all, values, sums, out, rms):
    chunks, _, rows, dim = values.shape
    whole = jnp.sum(jnp.sum(sums[...], axis=0), axis=1, keepdims=True)
    root = jnp.sqrt(whole / (n_all * chunks * rows * dim))
    rms[...] = root
    scale = jnp.broadcast_to(root, (8, dim))
    for chunk in range(chunks):
        for c in range(2):
            scaled = values[chunk, c].reshape(-1, 8, dim) / scale[None]
            out[c, pl.ds(chunk, rows, stride=chunks), :] = scaled.reshape(-1, dim)


def shards(n_outer, n_inner, state_vector, gate_matrices):
    dim = gate_matrices.shape[2]
    amp_count = state_vector.shape[3]
    rows = amp_count // dim
    passive = rows // dim
    chunks = passive if (dim // n_outer) % 8 == 0 else 1
    held = pltpu.VMEM((chunks, 2, rows // chunks, dim), jnp.float32)
    n_all = n_outer * n_inner
    dma = pltpu.SemaphoreType.DMA
    vmem = pl.BlockSpec(memory_space=pltpu.VMEM)
    hbm = pl.BlockSpec(memory_space=pltpu.HBM)
    anywhere = pl.BlockSpec(memory_space=pl.ANY)
    values, sums = pl.pallas_call(
        functools.partial(kernel, n_outer, n_inner, chunks),
        out_shape=(
            jax.ShapeDtypeStruct((chunks, 2, rows // chunks, dim), jnp.float32),
            jax.ShapeDtypeStruct((n_all, 1, dim), jnp.float32),
        ),
        in_specs=[hbm, hbm],
        out_specs=(anywhere, anywhere),
        scratch_shapes=[
            pltpu.VMEM((2, rows, dim), jnp.float32),
            pltpu.VMEM(gate_matrices.shape, jnp.float32),
        ]
        + [held] * 5
        + [pltpu.VMEM((1, dim), jnp.float32), dma((5,))]
        + [dma((chunks, n_outer))] * 4
        + [dma((chunks, n_inner))] * 2
        + [dma((n_all,))] * 2,
        compiler_params=pltpu.CompilerParams(
            collective_id=0, has_side_effects=True, vmem_limit_bytes=TRADE_LIMIT
        ),
    )(state_vector.reshape(2, rows, dim), gate_matrices)
    final_state, root = pl.pallas_call(
        functools.partial(finish, n_all),
        out_shape=(
            jax.ShapeDtypeStruct((2, rows, dim), jnp.float32),
            jax.ShapeDtypeStruct((1, 1), jnp.float32),
        ),
        in_specs=[vmem, vmem],
        out_specs=(vmem, vmem),
        compiler_params=pltpu.CompilerParams(vmem_limit_bytes=LIMIT),
    )(values, sums)
    return final_state.reshape(state_vector.shape), root.reshape(())


def solution(mesh):
    in_specs = (P(None, "outer", "inner", None), P())
    out_specs = (P(None, "outer", "inner", None), P())
    body = functools.partial(shards, mesh.shape["outer"], mesh.shape["inner"])
    return jax.shard_map(body, mesh=mesh, in_specs=in_specs, out_specs=out_specs, check_vma=False)
```

```python
import functools

import jax
import jax.numpy as jnp
from jax import lax
from jax.experimental import pallas as pl
from jax.experimental.pallas import tpu as pltpu
from jax.sharding import PartitionSpec as P

MESH = pl.DeviceIdType.MESH
TRADE_LIMIT = 56_150_000
LIMIT = 16 * 1024 * 1024


def halves(values):
    high = values.astype(jnp.bfloat16)
    low = (values - high.astype(jnp.float32)).astype(jnp.bfloat16)
    return high, low


def product(left, right, dims):
    def one(a, b):
        return lax.dot_general(a, b, (dims, ((), ())), preferred_element_type=jnp.float32)

    return one(left[0], right[0]) + (one(left[0], right[1]) + one(left[1], right[0]))


def complex_matrix(real, imag):
    top = jnp.concatenate([real, -imag], axis=1)
    bottom = jnp.concatenate([imag, real], axis=1)
    return halves(jnp.concatenate([top, bottom], axis=0))


def spread(position, count):
    return (position % 2) * (count // 2) + position // 2


def kernel(
    n_outer, n_inner, chunks, state_in, gates_in, held_c, sums,
    state, gates, sent_a, held_a, sent_b, held_b, sent_c, part, fetched,
    send_a, recv_a, send_b, recv_b, send_c, recv_c, send_s, recv_s,
):
    def fetch(at):
        if at == 0:
            return pltpu.make_async_copy(state_in, state, fetched.at[0])
        return pltpu.make_async_copy(gates_in.at[at - 1], gates.at[at - 1], fetched.at[at])

    for at in (0, 1, 4, 2, 3):
        fetch(at).start()
    dim = gates.shape[2]
    passive = state.shape[1] // dim
    sub = passive // chunks
    step = dim // chunks
    rows_outer = dim // n_outer * sub
    rows_inner = dim // n_inner * sub
    ratio = n_outer // n_inner
    n_all = n_outer * n_inner
    outer, inner = lax.axis_index("outer"), lax.axis_index("inner")
    me = outer * n_inner + inner

    def block(ref, chunk, at, rows):
        return ref.at[chunk, :, pl.ds(pl.multiple_of(at * rows, rows), rows), :]

    def remote(src, dst, send, recv, target):
        return pltpu.make_async_remote_copy(
            src_ref=src, dst_ref=dst, send_sem=send, recv_sem=recv,
            device_id=target, device_id_type=MESH,
        )

    far_first = sorted(range(n_outer), key=lambda k: abs(2 * k - n_outer))

    def everyone(act):
        if n_all > 64:

            def body(k, carry):
                one(act, k // n_inner, k % n_inner)
                return carry

            lax.fori_loop(1, n_all, body, 0)
            return
        for a in far_first:
            for b in range(n_inner):
                if a or b:
                    one(act, a, b)

    def one(act, a, b):
        ahead = ((outer + a) % n_outer, (inner + b) % n_inner)
        behind = ((outer + n_outer - a) % n_outer, (inner + n_inner - b) % n_inner)
        act(a * n_inner + b, ahead, behind)

    barrier = pltpu.get_barrier_semaphore()

    for k in range(1, n_outer):
        pl.semaphore_signal(
            barrier, inc=1, device_id=((outer + k) % n_outer, inner), device_id_type=MESH
        )
    for k in range(1, n_inner):
        pl.semaphore_signal(
            barrier, inc=1, device_id=(outer, (inner + k) % n_inner), device_id_type=MESH
        )

    def load(ref, chunk):
        return jnp.concatenate(
            [
                jnp.concatenate(
                    [ref[chunk, c, pl.ds(b, dim, stride=sub), :] for b in range(sub)], axis=1
                )
                for c in range(2)
            ],
            axis=0,
        )

    def store(ref, chunk, values):
        for c in range(2):
            for b in range(sub):
                ref[chunk, c, pl.ds(b, dim, stride=sub), :] = values[
                    c * dim : (c + 1) * dim, b * dim : (b + 1) * dim
                ]

    def low_gate(values):
        rows = values.shape[0] // 2
        matrix = complex_matrix(gates[3, 0], gates[3, 1])
        columns = []
        for b in range(values.shape[1] // dim):
            both = values[:, b * dim : (b + 1) * dim]
            wide = jnp.concatenate([both[:rows], both[rows:]], axis=1)
            wide = product(halves(wide), matrix, ((1,), (1,)))
            columns.append(jnp.concatenate([wide[:, :dim], wide[:, dim:]], axis=0))
        return jnp.concatenate(columns, axis=1)

    fetch(0).wait()
    fetch(1).wait()
    first = halves(
        jnp.concatenate(
            [
                jnp.concatenate(
                    [state[c, w * dim : (w + 1) * dim, :] for w in range(passive)], axis=1
                )
                for c in range(2)
            ],
            axis=0,
        )
    )

    def trade_a(chunk):
        for k in far_first[:-1]:
            to = (outer + k) % n_outer
            remote(
                block(sent_a, chunk, spread(to, n_outer), rows_outer),
                block(held_a, chunk, outer, rows_outer),
                send_a.at[chunk, to], recv_a.at[chunk, outer], (to, inner),
            ).start()
        pltpu.make_async_copy(
            block(sent_a, chunk, spread(outer, n_outer), rows_outer),
            block(held_a, chunk, outer, rows_outer),
            recv_a.at[chunk, outer],
        ).start()

    for chunk in range(chunks):
        pick = pl.ds(chunk, step, stride=chunks)
        matrix = complex_matrix(gates[0, 0, pick, :], gates[0, 1, pick, :])
        values = product(matrix, first, ((1,), (0,)))
        if chunk > 0:
            if chunk == 1:
                fetch(4).wait()
            values = low_gate(values)
        for c in range(2):
            for w in range(passive):
                sent_a[chunk, c, w * step : (w + 1) * step, :] = values[
                    c * step : (c + 1) * step, w * dim : (w + 1) * dim
                ]
        if chunk == 0:
            pl.semaphore_wait(barrier, n_outer + n_inner - 2)
        trade_a(chunk)

    fetch(2).wait()
    matrix = complex_matrix(gates[1, 0], gates[1, 1])
    mine = spread(outer, n_outer)
    column, within = mine // ratio, mine % ratio
    slot = inner * ratio + within
    for chunk in range(chunks):
        for k in range(n_outer):
            spot = block(held_a, chunk, k, rows_outer)
            remote(spot, spot, send_a.at[chunk, k], recv_a.at[chunk, k], (outer, inner)).wait_recv()
        values = halves(load(held_a, chunk))
        store(sent_b, chunk, product(matrix, values, ((1,), (0,))))
        for k in far_first:
            to = (outer + k) % n_outer
            src = block(sent_b, chunk, to, rows_outer)
            dst = block(held_b, chunk, slot, rows_outer)
            copy = remote(
                src, dst, send_b.at[chunk, to], recv_b.at[chunk, slot], (to, column)
            )
            if k > 0:
                copy.start()
            else:
                pl.when(column != inner)(copy.start)
                pl.when(column == inner)(
                    pltpu.make_async_copy(src, dst, recv_b.at[chunk, slot]).start
                )

    fetch(3).wait()
    matrix = complex_matrix(gates[2, 0], gates[2, 1])
    total = jnp.zeros((1, dim), jnp.float32)
    own = pltpu.make_async_copy(part, sums.at[me], recv_s.at[0])

    def share(k, ahead, behind):
        remote(part, sums.at[me], send_s.at[k], recv_s.at[k], ahead).start()

    for chunk in range(chunks):
        for k in range(n_outer):
            spot = block(held_b, chunk, k, rows_outer)
            remote(spot, spot, send_b.at[chunk, k], recv_b.at[chunk, k], (outer, inner)).wait_recv()
        values = product(matrix, halves(load(held_b, chunk)), ((1,), (0,)))
        if chunk == 0:
            if chunks == 1:
                fetch(4).wait()
            values = low_gate(values)
        for b in range(sub):
            piece = values[:, b * dim : (b + 1) * dim]
            total = total + jnp.sum(piece * piece, axis=0, keepdims=True)
        if chunk == chunks - 1:
            part[...] = total
            everyone(share)
            own.start()
        store(sent_c, chunk, values)
        for k in range(1, n_inner):
            to = (inner + k) % n_inner
            remote(
                block(sent_c, chunk, to, rows_inner),
                block(held_c, chunk, inner, rows_inner),
                send_c.at[chunk, to], recv_c.at[chunk, inner], (outer, to),
            ).start()
        pltpu.make_async_copy(
            block(sent_c, chunk, inner, rows_inner),
            block(held_c, chunk, inner, rows_inner),
            recv_c.at[chunk, inner],
        ).start()

    def arrived(k, ahead, behind):
        spot = sums.at[behind[0] * n_inner + behind[1]]
        remote(part, spot, send_s.at[k], recv_s.at[k], ahead).wait_recv()

    def left(k, ahead, behind):
        remote(part, sums.at[me], send_s.at[k], recv_s.at[k], ahead).wait_send()

    for chunk in range(chunks):
        for k in range(n_inner):
            spot = block(held_c, chunk, k, rows_inner)
            remote(spot, spot, send_c.at[chunk, k], recv_c.at[chunk, k], (outer, inner)).wait_recv()

    for chunk in range(chunks):
        for k in range(1, n_outer):
            to = (outer + k) % n_outer
            spot = block(sent_a, chunk, to, rows_outer)
            remote(spot, spot, send_a.at[chunk, to], recv_a.at[chunk, to], (to, inner)).wait_send()
        for k in range(n_outer):
            to = (outer + k) % n_outer
            spot = block(sent_b, chunk, to, rows_outer)
            copy = remote(spot, spot, send_b.at[chunk, to], recv_b.at[chunk, to], (to, column))
            if k > 0:
                copy.wait_send()
            else:
                pl.when(column != inner)(copy.wait_send)
        for k in range(1, n_inner):
            to = (inner + k) % n_inner
            spot = block(sent_c, chunk, to, rows_inner)
            remote(spot, spot, send_c.at[chunk, to], recv_c.at[chunk, to], (outer, to)).wait_send()
    everyone(left)
    own.wait()
    everyone(arrived)


def finish(n_all, values, sums, out, rms):
    chunks, _, rows, dim = values.shape
    whole = jnp.sum(jnp.sum(sums[...], axis=0), axis=1, keepdims=True)
    root = jnp.sqrt(whole / (n_all * chunks * rows * dim))
    rms[...] = root
    scale = jnp.broadcast_to(root, (8, dim))
    for chunk in range(chunks):
        for c in range(2):
            scaled = values[chunk, c].reshape(-1, 8, dim) / scale[None]
            out[c, pl.ds(chunk, rows, stride=chunks), :] = scaled.reshape(-1, dim)


def shards(n_outer, n_inner, state_vector, gate_matrices):
    dim = gate_matrices.shape[2]
    amp_count = state_vector.shape[3]
    rows = amp_count // dim
    passive = rows // dim
    chunks = passive if (dim // n_outer) % 8 == 0 else 1
    held = pltpu.VMEM((chunks, 2, rows // chunks, dim), jnp.float32)
    n_all = n_outer * n_inner
    dma = pltpu.SemaphoreType.DMA
    vmem = pl.BlockSpec(memory_space=pltpu.VMEM)
    hbm = pl.BlockSpec(memory_space=pltpu.HBM)
    anywhere = pl.BlockSpec(memory_space=pl.ANY)
    values, sums = pl.pallas_call(
        functools.partial(kernel, n_outer, n_inner, chunks),
        out_shape=(
            jax.ShapeDtypeStruct((chunks, 2, rows // chunks, dim), jnp.float32),
            jax.ShapeDtypeStruct((n_all, 1, dim), jnp.float32),
        ),
        in_specs=[hbm, hbm],
        out_specs=(anywhere, anywhere),
        scratch_shapes=[
            pltpu.VMEM((2, rows, dim), jnp.float32),
            pltpu.VMEM(gate_matrices.shape, jnp.float32),
        ]
        + [held] * 5
        + [pltpu.VMEM((1, dim), jnp.float32), dma((5,))]
        + [dma((chunks, n_outer))] * 4
        + [dma((chunks, n_inner))] * 2
        + [dma((n_all,))] * 2,
        compiler_params=pltpu.CompilerParams(
            collective_id=0, has_side_effects=True, vmem_limit_bytes=TRADE_LIMIT
        ),
    )(state_vector.reshape(2, rows, dim), gate_matrices)
    final_state, root = pl.pallas_call(
        functools.partial(finish, n_all),
        out_shape=(
            jax.ShapeDtypeStruct((2, rows, dim), jnp.float32),
            jax.ShapeDtypeStruct((1, 1), jnp.float32),
        ),
        in_specs=[vmem, vmem],
        out_specs=(vmem, vmem),
        compiler_params=pltpu.CompilerParams(vmem_limit_bytes=LIMIT),
    )(values, sums)
    return final_state.reshape(state_vector.shape), root.reshape(())


def solution(mesh):
    in_specs = (P(None, "outer", "inner", None), P())
    out_specs = (P(None, "outer", "inner", None), P())
    body = functools.partial(shards, mesh.shape["outer"], mesh.shape["inner"])
    return jax.shard_map(body, mesh=mesh, in_specs=in_specs, out_specs=out_specs, check_vma=False)
```

```python
import functools

import jax
import jax.numpy as jnp
from jax import lax
from jax.experimental import pallas as pl
from jax.experimental.pallas import tpu as pltpu
from jax.sharding import PartitionSpec as P

MESH = pl.DeviceIdType.MESH
TRADE_LIMIT = 56_150_000
LIMIT = 16 * 1024 * 1024


def halves(values):
    high = values.astype(jnp.bfloat16)
    low = (values - high.astype(jnp.float32)).astype(jnp.bfloat16)
    return high, low


def product(left, right, dims):
    def one(a, b):
        return lax.dot_general(a, b, (dims, ((), ())), preferred_element_type=jnp.float32)

    return one(left[0], right[0]) + (one(left[0], right[1]) + one(left[1], right[0]))


def complex_matrix(real, imag):
    top = jnp.concatenate([real, -imag], axis=1)
    bottom = jnp.concatenate([imag, real], axis=1)
    return halves(jnp.concatenate([top, bottom], axis=0))


def spread(position, count):
    half, rest = count // 2, position // 2
    return (position % 2) * half + (rest % 2) * (half // 2) + rest // 2


def kernel(
    n_outer, n_inner, chunks, state_in, gates_in, held_c, sums,
    state, gates, sent_a, held_a, sent_b, held_b, sent_c, part, fetched,
    send_a, recv_a, send_b, recv_b, send_c, recv_c, send_s, recv_s,
):
    def fetch(at):
        if at == 0:
            return pltpu.make_async_copy(state_in, state, fetched.at[0])
        return pltpu.make_async_copy(gates_in.at[at - 1], gates.at[at - 1], fetched.at[at])

    for at in (0, 1, 4, 2, 3):
        fetch(at).start()
    dim = gates.shape[2]
    passive = state.shape[1] // dim
    sub = passive // chunks
    step = dim // chunks
    rows_outer = dim // n_outer * sub
    rows_inner = dim // n_inner * sub
    ratio = n_outer // n_inner
    n_all = n_outer * n_inner
    outer, inner = lax.axis_index("outer"), lax.axis_index("inner")
    me = outer * n_inner + inner

    def block(ref, chunk, at, rows):
        return ref.at[chunk, :, pl.ds(pl.multiple_of(at * rows, rows), rows), :]

    def remote(src, dst, send, recv, target):
        return pltpu.make_async_remote_copy(
            src_ref=src, dst_ref=dst, send_sem=send, recv_sem=recv,
            device_id=target, device_id_type=MESH,
        )

    far_first = sorted(range(n_outer), key=lambda k: abs(2 * k - n_outer))

    def everyone(act):
        if n_all > 64:

            def body(k, carry):
                one(act, k // n_inner, k % n_inner)
                return carry

            lax.fori_loop(1, n_all, body, 0)
            return
        for a in far_first:
            for b in range(n_inner):
                if a or b:
                    one(act, a, b)

    def one(act, a, b):
        ahead = ((outer + a) % n_outer, (inner + b) % n_inner)
        behind = ((outer + n_outer - a) % n_outer, (inner + n_inner - b) % n_inner)
        act(a * n_inner + b, ahead, behind)

    barrier = pltpu.get_barrier_semaphore()

    for k in range(1, n_outer):
        pl.semaphore_signal(
            barrier, inc=1, device_id=((outer + k) % n_outer, inner), device_id_type=MESH
        )
    for k in range(1, n_inner):
        pl.semaphore_signal(
            barrier, inc=1, device_id=(outer, (inner + k) % n_inner), device_id_type=MESH
        )

    def load(ref, chunk):
        return jnp.concatenate(
            [
                jnp.concatenate(
                    [ref[chunk, c, pl.ds(b, dim, stride=sub), :] for b in range(sub)], axis=1
                )
                for c in range(2)
            ],
            axis=0,
        )

    def store(ref, chunk, values):
        for c in range(2):
            for b in range(sub):
                ref[chunk, c, pl.ds(b, dim, stride=sub), :] = values[
                    c * dim : (c + 1) * dim, b * dim : (b + 1) * dim
                ]

    def low_gate(values):
        rows = values.shape[0] // 2
        matrix = complex_matrix(gates[3, 0], gates[3, 1])
        columns = []
        for b in range(values.shape[1] // dim):
            both = values[:, b * dim : (b + 1) * dim]
            wide = jnp.concatenate([both[:rows], both[rows:]], axis=1)
            wide = product(halves(wide), matrix, ((1,), (1,)))
            columns.append(jnp.concatenate([wide[:, :dim], wide[:, dim:]], axis=0))
        return jnp.concatenate(columns, axis=1)

    fetch(0).wait()
    fetch(1).wait()
    first = halves(
        jnp.concatenate(
            [
                jnp.concatenate(
                    [state[c, w * dim : (w + 1) * dim, :] for w in range(passive)], axis=1
                )
                for c in range(2)
            ],
            axis=0,
        )
    )

    def trade_a(chunk):
        for k in far_first[:-1]:
            to = (outer + k) % n_outer
            remote(
                block(sent_a, chunk, spread(to, n_outer), rows_outer),
                block(held_a, chunk, outer, rows_outer),
                send_a.at[chunk, to], recv_a.at[chunk, outer], (to, inner),
            ).start()
        pltpu.make_async_copy(
            block(sent_a, chunk, spread(outer, n_outer), rows_outer),
            block(held_a, chunk, outer, rows_outer),
            recv_a.at[chunk, outer],
        ).start()

    for chunk in range(chunks):
        pick = pl.ds(chunk, step, stride=chunks)
        matrix = complex_matrix(gates[0, 0, pick, :], gates[0, 1, pick, :])
        values = product(matrix, first, ((1,), (0,)))
        if chunk > 0:
            if chunk == 1:
                fetch(4).wait()
            values = low_gate(values)
        for c in range(2):
            for w in range(passive):
                sent_a[chunk, c, w * step : (w + 1) * step, :] = values[
                    c * step : (c + 1) * step, w * dim : (w + 1) * dim
                ]
        if chunk == 0:
            pl.semaphore_wait(barrier, n_outer + n_inner - 2)
        trade_a(chunk)

    fetch(2).wait()
    matrix = complex_matrix(gates[1, 0], gates[1, 1])
    mine = spread(outer, n_outer)
    column, within = mine // ratio, mine % ratio
    slot = inner * ratio + within
    for chunk in range(chunks):
        for k in range(n_outer):
            spot = block(held_a, chunk, k, rows_outer)
            remote(spot, spot, send_a.at[chunk, k], recv_a.at[chunk, k], (outer, inner)).wait_recv()
        values = halves(load(held_a, chunk))
        store(sent_b, chunk, product(matrix, values, ((1,), (0,))))
        for k in far_first:
            to = (outer + k) % n_outer
            src = block(sent_b, chunk, to, rows_outer)
            dst = block(held_b, chunk, slot, rows_outer)
            copy = remote(
                src, dst, send_b.at[chunk, to], recv_b.at[chunk, slot], (to, column)
            )
            if k > 0:
                copy.start()
            else:
                pl.when(column != inner)(copy.start)
                pl.when(column == inner)(
                    pltpu.make_async_copy(src, dst, recv_b.at[chunk, slot]).start
                )

    fetch(3).wait()
    matrix = complex_matrix(gates[2, 0], gates[2, 1])
    total = jnp.zeros((1, dim), jnp.float32)
    own = pltpu.make_async_copy(part, sums.at[me], recv_s.at[0])

    def share(k, ahead, behind):
        remote(part, sums.at[me], send_s.at[k], recv_s.at[k], ahead).start()

    for chunk in range(chunks):
        for k in range(n_outer):
            spot = block(held_b, chunk, k, rows_outer)
            remote(spot, spot, send_b.at[chunk, k], recv_b.at[chunk, k], (outer, inner)).wait_recv()
        values = product(matrix, halves(load(held_b, chunk)), ((1,), (0,)))
        if chunk == 0:
            if chunks == 1:
                fetch(4).wait()
            values = low_gate(values)
        for b in range(sub):
            piece = values[:, b * dim : (b + 1) * dim]
            total = total + jnp.sum(piece * piece, axis=0, keepdims=True)
        if chunk == chunks - 1:
            part[...] = total
            everyone(share)
            own.start()
        store(sent_c, chunk, values)
        for k in range(1, n_inner):
            to = (inner + k) % n_inner
            remote(
                block(sent_c, chunk, to, rows_inner),
                block(held_c, chunk, inner, rows_inner),
                send_c.at[chunk, to], recv_c.at[chunk, inner], (outer, to),
            ).start()
        pltpu.make_async_copy(
            block(sent_c, chunk, inner, rows_inner),
            block(held_c, chunk, inner, rows_inner),
            recv_c.at[chunk, inner],
        ).start()

    def arrived(k, ahead, behind):
        spot = sums.at[behind[0] * n_inner + behind[1]]
        remote(part, spot, send_s.at[k], recv_s.at[k], ahead).wait_recv()

    def left(k, ahead, behind):
        remote(part, sums.at[me], send_s.at[k], recv_s.at[k], ahead).wait_send()

    for chunk in range(chunks):
        for k in range(n_inner):
            spot = block(held_c, chunk, k, rows_inner)
            remote(spot, spot, send_c.at[chunk, k], recv_c.at[chunk, k], (outer, inner)).wait_recv()

    for chunk in range(chunks):
        for k in range(1, n_outer):
            to = (outer + k) % n_outer
            spot = block(sent_a, chunk, to, rows_outer)
            remote(spot, spot, send_a.at[chunk, to], recv_a.at[chunk, to], (to, inner)).wait_send()
        for k in range(n_outer):
            to = (outer + k) % n_outer
            spot = block(sent_b, chunk, to, rows_outer)
            copy = remote(spot, spot, send_b.at[chunk, to], recv_b.at[chunk, to], (to, column))
            if k > 0:
                copy.wait_send()
            else:
                pl.when(column != inner)(copy.wait_send)
        for k in range(1, n_inner):
            to = (inner + k) % n_inner
            spot = block(sent_c, chunk, to, rows_inner)
            remote(spot, spot, send_c.at[chunk, to], recv_c.at[chunk, to], (outer, to)).wait_send()
    everyone(left)
    own.wait()
    everyone(arrived)


def finish(n_all, values, sums, out, rms):
    chunks, _, rows, dim = values.shape
    whole = jnp.sum(jnp.sum(sums[...], axis=0), axis=1, keepdims=True)
    root = jnp.sqrt(whole / (n_all * chunks * rows * dim))
    rms[...] = root
    scale = jnp.broadcast_to(1.0 / root, (8, dim))
    for chunk in range(chunks):
        for c in range(2):
            scaled = values[chunk, c].reshape(-1, 8, dim) * scale[None]
            out[c, pl.ds(chunk, rows, stride=chunks), :] = scaled.reshape(-1, dim)


def shards(n_outer, n_inner, state_vector, gate_matrices):
    dim = gate_matrices.shape[2]
    amp_count = state_vector.shape[3]
    rows = amp_count // dim
    passive = rows // dim
    chunks = passive if (dim // n_outer) % 8 == 0 else 1
    held = pltpu.VMEM((chunks, 2, rows // chunks, dim), jnp.float32)
    n_all = n_outer * n_inner
    dma = pltpu.SemaphoreType.DMA
    vmem = pl.BlockSpec(memory_space=pltpu.VMEM)
    hbm = pl.BlockSpec(memory_space=pltpu.HBM)
    anywhere = pl.BlockSpec(memory_space=pl.ANY)
    values, sums = pl.pallas_call(
        functools.partial(kernel, n_outer, n_inner, chunks),
        out_shape=(
            jax.ShapeDtypeStruct((chunks, 2, rows // chunks, dim), jnp.float32),
            jax.ShapeDtypeStruct((n_all, 1, dim), jnp.float32),
        ),
        in_specs=[hbm, hbm],
        out_specs=(anywhere, anywhere),
        scratch_shapes=[
            pltpu.VMEM((2, rows, dim), jnp.float32),
            pltpu.VMEM(gate_matrices.shape, jnp.float32),
        ]
        + [held] * 5
        + [pltpu.VMEM((1, dim), jnp.float32), dma((5,))]
        + [dma((chunks, n_outer))] * 4
        + [dma((chunks, n_inner))] * 2
        + [dma((n_all,))] * 2,
        compiler_params=pltpu.CompilerParams(
            collective_id=0, has_side_effects=True, vmem_limit_bytes=TRADE_LIMIT
        ),
    )(state_vector.reshape(2, rows, dim), gate_matrices)
    final_state, root = pl.pallas_call(
        functools.partial(finish, n_all),
        out_shape=(
            jax.ShapeDtypeStruct((2, rows, dim), jnp.float32),
            jax.ShapeDtypeStruct((1, 1), jnp.float32),
        ),
        in_specs=[vmem, vmem],
        out_specs=(vmem, vmem),
        compiler_params=pltpu.CompilerParams(vmem_limit_bytes=LIMIT),
    )(values, sums)
    return final_state.reshape(state_vector.shape), root.reshape(())


def solution(mesh):
    in_specs = (P(None, "outer", "inner", None), P())
    out_specs = (P(None, "outer", "inner", None), P())
    body = functools.partial(shards, mesh.shape["outer"], mesh.shape["inner"])
    return jax.shard_map(body, mesh=mesh, in_specs=in_specs, out_specs=out_specs, check_vma=False)
```

```python
import functools

import jax
import jax.numpy as jnp
from jax import lax
from jax.experimental import pallas as pl
from jax.experimental.pallas import tpu as pltpu
from jax.sharding import PartitionSpec as P

MESH = pl.DeviceIdType.MESH
TRADE_LIMIT = 56_150_000
LIMIT = 16 * 1024 * 1024


def halves(values):
    high = values.astype(jnp.bfloat16)
    low = (values - high.astype(jnp.float32)).astype(jnp.bfloat16)
    return high, low


def product(left, right, dims):
    def one(a, b):
        return lax.dot_general(a, b, (dims, ((), ())), preferred_element_type=jnp.float32)

    return one(left[0], right[0]) + (one(left[0], right[1]) + one(left[1], right[0]))


def complex_matrix(real, imag):
    top = jnp.concatenate([real, -imag], axis=1)
    bottom = jnp.concatenate([imag, real], axis=1)
    return halves(jnp.concatenate([top, bottom], axis=0))


def spread(position, count):
    half, rest = count // 2, position // 2
    return (rest % 2) * half + (position % 2) * (half // 2) + rest // 2


def kernel(
    n_outer, n_inner, chunks, state_in, gates_in, held_c, sums,
    state, gates, sent_a, held_a, sent_b, held_b, sent_c, part, fetched,
    send_a, recv_a, send_b, recv_b, send_c, recv_c, send_s, recv_s,
):
    def fetch(at):
        if at == 0:
            return pltpu.make_async_copy(state_in, state, fetched.at[0])
        return pltpu.make_async_copy(gates_in.at[at - 1], gates.at[at - 1], fetched.at[at])

    for at in (0, 1, 4, 2, 3):
        fetch(at).start()
    dim = gates.shape[2]
    passive = state.shape[1] // dim
    sub = passive // chunks
    step = dim // chunks
    rows_outer = dim // n_outer * sub
    rows_inner = dim // n_inner * sub
    ratio = n_outer // n_inner
    n_all = n_outer * n_inner
    outer, inner = lax.axis_index("outer"), lax.axis_index("inner")
    me = outer * n_inner + inner

    def block(ref, chunk, at, rows):
        return ref.at[chunk, :, pl.ds(pl.multiple_of(at * rows, rows), rows), :]

    def remote(src, dst, send, recv, target):
        return pltpu.make_async_remote_copy(
            src_ref=src, dst_ref=dst, send_sem=send, recv_sem=recv,
            device_id=target, device_id_type=MESH,
        )

    far_first = sorted(range(n_outer), key=lambda k: abs(2 * k - n_outer))

    def everyone(act):
        if n_all > 64:

            def body(k, carry):
                one(act, k // n_inner, k % n_inner)
                return carry

            lax.fori_loop(1, n_all, body, 0)
            return
        for a in far_first:
            for b in range(n_inner):
                if a or b:
                    one(act, a, b)

    def one(act, a, b):
        ahead = ((outer + a) % n_outer, (inner + b) % n_inner)
        behind = ((outer + n_outer - a) % n_outer, (inner + n_inner - b) % n_inner)
        act(a * n_inner + b, ahead, behind)

    barrier = pltpu.get_barrier_semaphore()

    for k in range(1, n_outer):
        pl.semaphore_signal(
            barrier, inc=1, device_id=((outer + k) % n_outer, inner), device_id_type=MESH
        )
    for k in range(1, n_inner):
        pl.semaphore_signal(
            barrier, inc=1, device_id=(outer, (inner + k) % n_inner), device_id_type=MESH
        )

    def load(ref, chunk):
        return jnp.concatenate(
            [
                jnp.concatenate(
                    [ref[chunk, c, pl.ds(b, dim, stride=sub), :] for b in range(sub)], axis=1
                )
                for c in range(2)
            ],
            axis=0,
        )

    def store(ref, chunk, values):
        for c in range(2):
            for b in range(sub):
                ref[chunk, c, pl.ds(b, dim, stride=sub), :] = values[
                    c * dim : (c + 1) * dim, b * dim : (b + 1) * dim
                ]

    def low_gate(values):
        rows = values.shape[0] // 2
        matrix = complex_matrix(gates[3, 0], gates[3, 1])
        columns = []
        for b in range(values.shape[1] // dim):
            both = values[:, b * dim : (b + 1) * dim]
            wide = jnp.concatenate([both[:rows], both[rows:]], axis=1)
            wide = product(halves(wide), matrix, ((1,), (1,)))
            columns.append(jnp.concatenate([wide[:, :dim], wide[:, dim:]], axis=0))
        return jnp.concatenate(columns, axis=1)

    fetch(0).wait()
    fetch(1).wait()
    first = halves(
        jnp.concatenate(
            [
                jnp.concatenate(
                    [state[c, w * dim : (w + 1) * dim, :] for w in range(passive)], axis=1
                )
                for c in range(2)
            ],
            axis=0,
        )
    )

    def trade_a(chunk):
        for k in far_first[:-1]:
            to = (outer + k) % n_outer
            remote(
                block(sent_a, chunk, spread(to, n_outer), rows_outer),
                block(held_a, chunk, outer, rows_outer),
                send_a.at[chunk, to], recv_a.at[chunk, outer], (to, inner),
            ).start()
        pltpu.make_async_copy(
            block(sent_a, chunk, spread(outer, n_outer), rows_outer),
            block(held_a, chunk, outer, rows_outer),
            recv_a.at[chunk, outer],
        ).start()

    for chunk in range(chunks):
        pick = pl.ds(chunk, step, stride=chunks)
        matrix = complex_matrix(gates[0, 0, pick, :], gates[0, 1, pick, :])
        values = product(matrix, first, ((1,), (0,)))
        if chunk > 0:
            if chunk == 1:
                fetch(4).wait()
            values = low_gate(values)
        for c in range(2):
            for w in range(passive):
                sent_a[chunk, c, w * step : (w + 1) * step, :] = values[
                    c * step : (c + 1) * step, w * dim : (w + 1) * dim
                ]
        if chunk == 0:
            pl.semaphore_wait(barrier, n_outer + n_inner - 2)
        trade_a(chunk)

    fetch(2).wait()
    matrix = complex_matrix(gates[1, 0], gates[1, 1])
    mine = spread(outer, n_outer)
    column, within = mine // ratio, mine % ratio
    slot = inner * ratio + within
    for chunk in range(chunks):
        for k in range(n_outer):
            spot = block(held_a, chunk, k, rows_outer)
            remote(spot, spot, send_a.at[chunk, k], recv_a.at[chunk, k], (outer, inner)).wait_recv()
        values = halves(load(held_a, chunk))
        store(sent_b, chunk, product(matrix, values, ((1,), (0,))))
        for k in far_first:
            to = (outer + k) % n_outer
            src = block(sent_b, chunk, to, rows_outer)
            dst = block(held_b, chunk, slot, rows_outer)
            copy = remote(
                src, dst, send_b.at[chunk, to], recv_b.at[chunk, slot], (to, column)
            )
            if k > 0:
                copy.start()
            else:
                pl.when(column != inner)(copy.start)
                pl.when(column == inner)(
                    pltpu.make_async_copy(src, dst, recv_b.at[chunk, slot]).start
                )

    fetch(3).wait()
    matrix = complex_matrix(gates[2, 0], gates[2, 1])
    total = jnp.zeros((1, dim), jnp.float32)
    own = pltpu.make_async_copy(part, sums.at[me], recv_s.at[0])

    def share(k, ahead, behind):
        remote(part, sums.at[me], send_s.at[k], recv_s.at[k], ahead).start()

    for chunk in range(chunks):
        for k in range(n_outer):
            spot = block(held_b, chunk, k, rows_outer)
            remote(spot, spot, send_b.at[chunk, k], recv_b.at[chunk, k], (outer, inner)).wait_recv()
        values = product(matrix, halves(load(held_b, chunk)), ((1,), (0,)))
        if chunk == 0:
            if chunks == 1:
                fetch(4).wait()
            values = low_gate(values)
        for b in range(sub):
            piece = values[:, b * dim : (b + 1) * dim]
            total = total + jnp.sum(piece * piece, axis=0, keepdims=True)
        if chunk == chunks - 1:
            part[...] = total
            everyone(share)
            own.start()
        store(sent_c, chunk, values)
        for k in range(1, n_inner):
            to = (inner + k) % n_inner
            remote(
                block(sent_c, chunk, to, rows_inner),
                block(held_c, chunk, inner, rows_inner),
                send_c.at[chunk, to], recv_c.at[chunk, inner], (outer, to),
            ).start()
        pltpu.make_async_copy(
            block(sent_c, chunk, inner, rows_inner),
            block(held_c, chunk, inner, rows_inner),
            recv_c.at[chunk, inner],
        ).start()

    def arrived(k, ahead, behind):
        spot = sums.at[behind[0] * n_inner + behind[1]]
        remote(part, spot, send_s.at[k], recv_s.at[k], ahead).wait_recv()

    def left(k, ahead, behind):
        remote(part, sums.at[me], send_s.at[k], recv_s.at[k], ahead).wait_send()

    for chunk in range(chunks):
        for k in range(n_inner):
            spot = block(held_c, chunk, k, rows_inner)
            remote(spot, spot, send_c.at[chunk, k], recv_c.at[chunk, k], (outer, inner)).wait_recv()

    for chunk in range(chunks):
        for k in range(1, n_outer):
            to = (outer + k) % n_outer
            spot = block(sent_a, chunk, to, rows_outer)
            remote(spot, spot, send_a.at[chunk, to], recv_a.at[chunk, to], (to, inner)).wait_send()
        for k in range(n_outer):
            to = (outer + k) % n_outer
            spot = block(sent_b, chunk, to, rows_outer)
            copy = remote(spot, spot, send_b.at[chunk, to], recv_b.at[chunk, to], (to, column))
            if k > 0:
                copy.wait_send()
            else:
                pl.when(column != inner)(copy.wait_send)
        for k in range(1, n_inner):
            to = (inner + k) % n_inner
            spot = block(sent_c, chunk, to, rows_inner)
            remote(spot, spot, send_c.at[chunk, to], recv_c.at[chunk, to], (outer, to)).wait_send()
    everyone(left)
    own.wait()
    everyone(arrived)


def finish(n_all, values, sums, out, rms):
    chunks, _, rows, dim = values.shape
    whole = jnp.sum(jnp.sum(sums[...], axis=0), axis=1, keepdims=True)
    root = jnp.sqrt(whole / (n_all * chunks * rows * dim))
    rms[...] = root
    scale = jnp.broadcast_to(1.0 / root, (8, dim))
    for chunk in range(chunks):
        for c in range(2):
            scaled = values[chunk, c].reshape(-1, 8, dim) * scale[None]
            out[c, pl.ds(chunk, rows, stride=chunks), :] = scaled.reshape(-1, dim)


def shards(n_outer, n_inner, state_vector, gate_matrices):
    dim = gate_matrices.shape[2]
    amp_count = state_vector.shape[3]
    rows = amp_count // dim
    passive = rows // dim
    chunks = passive if (dim // n_outer) % 8 == 0 else 1
    held = pltpu.VMEM((chunks, 2, rows // chunks, dim), jnp.float32)
    n_all = n_outer * n_inner
    dma = pltpu.SemaphoreType.DMA
    vmem = pl.BlockSpec(memory_space=pltpu.VMEM)
    hbm = pl.BlockSpec(memory_space=pltpu.HBM)
    anywhere = pl.BlockSpec(memory_space=pl.ANY)
    values, sums = pl.pallas_call(
        functools.partial(kernel, n_outer, n_inner, chunks),
        out_shape=(
            jax.ShapeDtypeStruct((chunks, 2, rows // chunks, dim), jnp.float32),
            jax.ShapeDtypeStruct((n_all, 1, dim), jnp.float32),
        ),
        in_specs=[hbm, hbm],
        out_specs=(anywhere, anywhere),
        scratch_shapes=[
            pltpu.VMEM((2, rows, dim), jnp.float32),
            pltpu.VMEM(gate_matrices.shape, jnp.float32),
        ]
        + [held] * 5
        + [pltpu.VMEM((1, dim), jnp.float32), dma((5,))]
        + [dma((chunks, n_outer))] * 4
        + [dma((chunks, n_inner))] * 2
        + [dma((n_all,))] * 2,
        compiler_params=pltpu.CompilerParams(
            collective_id=0, has_side_effects=True, vmem_limit_bytes=TRADE_LIMIT
        ),
    )(state_vector.reshape(2, rows, dim), gate_matrices)
    final_state, root = pl.pallas_call(
        functools.partial(finish, n_all),
        out_shape=(
            jax.ShapeDtypeStruct((2, rows, dim), jnp.float32),
            jax.ShapeDtypeStruct((1, 1), jnp.float32),
        ),
        in_specs=[vmem, vmem],
        out_specs=(vmem, vmem),
        compiler_params=pltpu.CompilerParams(vmem_limit_bytes=LIMIT),
    )(values, sums)
    return final_state.reshape(state_vector.shape), root.reshape(())


def solution(mesh):
    in_specs = (P(None, "outer", "inner", None), P())
    out_specs = (P(None, "outer", "inner", None), P())
    body = functools.partial(shards, mesh.shape["outer"], mesh.shape["inner"])
    return jax.shard_map(body, mesh=mesh, in_specs=in_specs, out_specs=out_specs, check_vma=False)
```
